32 devices in a mesh: grp: 2 (over y), ka: 4 (over z), ga: 2 (over x), ba: 2 (over core).
Axes of the slice: x: 2, y: 2, z: 4, core: 2. Of those that a mesh axis runs over, the one named last changes fastest.
Arguments:
- coefficients: bfloat16 [2, 2, 16, 512, 9216], P(None, None, ('grp', 'ka'), 'ba', 'ga'), parts along dimension 2, may hold values from -1 to 1
- occupied: int32 [2, 16], P(None, ('grp', 'ka')), parts along dimension 1, may hold values from 64 to 512
- kweights: float32 [16], P(('grp', 'ka')), parts along dimension 0, may hold values from 0.5 to 2
- owner_map: int32 [1024], P('grp'), parts along dimension 0, may hold values from 0 to 7, as said below
- species: int32 [1024], P('grp'), parts along dimension 0, may hold values from 0 to 1
- positions: float32 [3, 1024], P(None, 'grp'), parts along dimension 1, may hold values from 0 to 100
- multipole: float32 [2, 9, 324], replicated, may hold values from -0.3125 to 0.3125
- widths: float32 [2], replicated, may hold values from 0.05 to 0.3
- potential: float32 [2, 442368], P(None, ('grp', 'ga')), parts along dimension 1, may hold values from -0.013671875 to 0.013671875
Outputs:
- density: float32 [2, 2, 1024, 324], P(None, None, ('grp', 'ka', 'ga', 'ba')), parts along dimension 2
- forces: float32 [3, 1024], P(None, ('grp', 'ka', 'ga', 'ba')), parts along dimension 1
The draws below stay inside these ranges and needn't reach their ends.
There are 2 independent parts, one for each index of `grp`. The reference program is written for one: setup_inputs(seed, part) draws one part's arguments, and reference() takes and returns one part's arrays. A program takes and returns all parts, laid end to end along the dimension named above; an argument that names none is the same for every part. Nothing has to cross between parts.
Inputs may be any that keep to these rules, and one draw needn't show every extreme that they name: `owner_map`: within each aligned block of 256 atoms every owner number is named by exactly 32 atoms.
All inputs are finite; a program needn't handle non-finite values.
Results may differ from the reference program's by a relative error of at most 0.0003.
Values sent between devices are 32-bit elements; how exact they have to be, the bound alone decides.
A program may use at most 192 MiB of HBM per device.

```python
import math
import jax
import jax.numpy as jnp
from jax import lax

NSPIN = 2
NPROJ = 18
ATOMS = 512
SPECIES = 2
NL = 9
GRID = 96
G_DEV = 110592
KPTS = 8
BANDS = 512
GTOT = 221184
ATOMS_BLK = 256
PER_OWN = 32
N_GA = 2
N_BA = 2


def draw_coefficients(key, part):
    keys = jax.random.split(key, 4)
    dims_all = (NSPIN, KPTS, BANDS, ATOMS, NPROJ)
    spread = (KPTS * BANDS) ** (-0.5)
    real_noise = jax.random.normal(keys[0], dims_all, jnp.float32)
    imag_noise = jax.random.normal(keys[1], dims_all, jnp.float32)
    mix_real = jax.random.normal(keys[2], (ATOMS, NPROJ, NPROJ), jnp.float32) / 6.0
    mix_imag = jax.random.normal(keys[3], (ATOMS, NPROJ, NPROJ), jnp.float32) / 6.0
    real_part = spread * (jnp.einsum('skbai,aij->skbaj', real_noise, mix_real) - jnp.einsum('skbai,aij->skbaj', imag_noise, mix_imag))
    imag_part = spread * (jnp.einsum('skbai,aij->skbaj', real_noise, mix_imag) + jnp.einsum('skbai,aij->skbaj', imag_noise, mix_real))
    stacked = jnp.stack([real_part, imag_part], axis=1).reshape(NSPIN, 2, KPTS, BANDS, ATOMS * NPROJ)
    return jnp.clip(stacked, -1.0, 1.0).astype(jnp.bfloat16)


def draw_owner_map(key, part):
    blocks = ATOMS // ATOMS_BLK

    def one_block(number):
        return jax.random.permutation(jax.random.fold_in(key, number), ATOMS_BLK)
    shuffled = jax.vmap(one_block)(jnp.arange(blocks, dtype=jnp.int32))
    return (shuffled // PER_OWN).reshape(ATOMS).astype(jnp.int32)


def place_ends(values, key, least, high):
    shape = values.shape
    index_at = [jax.random.randint(jax.random.fold_in(key, axis), (), 0, shape[axis]) for axis in range(len(shape))]
    values = values.at[tuple(index_at)].set(least)
    longest = shape.index(max(shape))
    index_at[longest] = (index_at[longest] + 1) % shape[longest]
    return values.at[tuple(index_at)].set(high)


def block_scale(stream_key, extent, cuts, smallest, high):
    gain, own = 1.0, jax.random.fold_in(stream_key, 6)
    for axis_at, parts in cuts:
        steps = jnp.exp(jax.random.uniform(jax.random.fold_in(own, axis_at), (parts,), jnp.float32, smallest / len(cuts), high / len(cuts)))
        gain = gain * jnp.repeat(steps, extent[axis_at] // parts).reshape([-1 if axis == axis_at else 1 for axis in range(len(extent))])
    return gain


def centred(rng, shape, width, reach, shards=(), kind=jnp.bfloat16):
    factor_of = block_scale(rng, shape, shards, -0.22, 0.18) if shards else 1.0
    array = jax.random.normal(rng, shape, jnp.float32) * width * factor_of
    return jnp.minimum(jnp.maximum(array, -reach), reach).astype(kind)


def setup_inputs(seed: int = 0, part: int = 0) -> dict:
    streams_of = jax.random.split(jax.random.key(seed), 10)
    part_splits = jax.random.split(jax.random.fold_in(streams_of[9], part), 10)
    return {
        "coefficients": draw_coefficients(jax.random.fold_in(jax.random.fold_in(streams_of[9], part), 71), part),
        "occupied": place_ends(jax.random.randint(part_splits[1], (NSPIN, KPTS), BANDS // 8, BANDS + 1), jax.random.fold_in(part_splits[1], 1), BANDS // 8, BANDS).astype(jnp.int32),
        "kweights": jnp.clip(jnp.exp(math.log(2.0) - 1.3862944 * jax.random.uniform(part_splits[2], (KPTS,), jnp.float32) ** block_scale(part_splits[2], (KPTS,), ((0, 4),), -0.2, 0.2)), 0.5, 2.0),
        "owner_map": draw_owner_map(jax.random.fold_in(jax.random.fold_in(streams_of[9], part), 71), part),
        "species": place_ends(jax.random.randint(part_splits[4], (ATOMS,), 0, SPECIES), jax.random.fold_in(part_splits[4], 1), 0, SPECIES - 1).astype(jnp.int32),
        "positions": jnp.clip(jax.random.uniform(part_splits[5], (3, ATOMS), jnp.float32, 0.0, 100.0), 0.0, 100.0),
        "multipole": centred(streams_of[6], (SPECIES, NL, NPROJ * NPROJ), (NPROJ * NPROJ) ** -0.5, 0.3125, (), jnp.float32),
        "widths": jnp.clip(jnp.exp(jax.random.uniform(streams_of[7], (SPECIES,), jnp.float32, math.log(0.05), math.log(0.3))), 0.05, 0.3),
        "potential": centred(part_splits[8], (2, GTOT), GTOT ** -0.5, 0.013671875, ((1, 2),), jnp.float32),
    }


grid_step = 0.0625
highest = lax.Precision.HIGHEST


def harmonics(start_index, length, widths):
    indices = start_index + jnp.arange(length, dtype=jnp.int32)
    planes = [indices % GRID, (indices // GRID) % GRID, indices // (GRID * GRID)]
    vectors = []
    for plane_index in planes:
        signed = jnp.where(plane_index >= GRID // 2, plane_index - GRID, plane_index)
        vectors.append(grid_step * signed.astype(jnp.float32))
    along_x, along_y, along_z = vectors
    square = along_x * along_x + along_y * along_y + along_z * along_z
    shapes = jnp.stack([jnp.ones_like(square), along_x, along_y, along_z, along_x * along_y, along_y * along_z, along_z * along_x, along_x * along_x - along_y * along_y, 3.0 * along_z * along_z - square])
    damping = jnp.exp(-widths[:, None] * square[None, :])
    form_table = (damping[:, None, :] * shapes[None, :, :]).reshape(SPECIES * NL, length)
    return form_table, jnp.stack(vectors, axis=1)


def force_block(moments, places, form_table, vectors, pot_piece):
    smooth = jnp.dot(moments, form_table, precision=highest)
    phases = jnp.dot(places, vectors.T, precision=highest)
    wave_term = pot_piece[0][None, :] * jnp.sin(phases) + pot_piece[1][None, :] * jnp.cos(phases)
    return jnp.dot(smooth * wave_term, vectors, precision=highest)


def reference(coefficients, occupied, kweights, owner_map, species, positions, multipole, widths, potential):
    band_index = jnp.arange(BANDS, dtype=jnp.int32)
    band_masks = (band_index[None, None, :] < occupied[:, :, None]).astype(jnp.float32)

    def kpoint(running, inputs):
        kpoint_slab, band_mask, weight = inputs
        values = kpoint_slab.astype(jnp.float32).reshape(NSPIN, 2, BANDS, ATOMS, NPROJ)
        masked = values * band_mask[:, None, :, None, None]
        real_part = jnp.einsum("scnai,scnaj->saij", values, masked)
        cross_term = jnp.einsum("snai,snaj->saij", values[:, 0], masked[:, 1])
        imag_part = cross_term - jnp.swapaxes(cross_term, 2, 3)
        return running + weight * jnp.stack([real_part, imag_part], axis=1), None

    initial = jnp.zeros((NSPIN, 2, ATOMS, NPROJ, NPROJ), jnp.float32)
    density_all, unused = lax.scan(kpoint, initial, (jnp.moveaxis(coefficients, 2, 0), jnp.moveaxis(band_masks, 1, 0), kweights))
    density_all = density_all.reshape(NSPIN, 2, ATOMS, NPROJ * NPROJ)
    atom_index = jnp.arange(ATOMS, dtype=jnp.int32)
    sort_key = ((owner_map // N_BA) * N_GA + atom_index // ATOMS_BLK) * N_BA + owner_map % N_BA
    ordering = jnp.argsort(sort_key, stable=True).astype(jnp.int32)
    density = jnp.take(density_all, ordering, axis=2)
    real_total = jnp.sum(density_all[:, 0], axis=0)
    selector = (species[:, None] == jnp.arange(SPECIES, dtype=jnp.int32)[None, :]).astype(jnp.float32)
    moments = jnp.dot(real_total, multipole.reshape(SPECIES * NL, NPROJ * NPROJ).T, precision=highest) * jnp.repeat(selector, NL, axis=1)
    block_size = G_DEV // 8
    places = positions.T

    def gblock(running, number):
        start_index = number * block_size
        form_table, vectors = harmonics(start_index, block_size, widths)
        pot_piece = lax.dynamic_slice_in_dim(potential, start_index, block_size, 1)
        return running + force_block(moments, places, form_table, vectors, pot_piece), None

    force_all, unused = lax.scan(gblock, jnp.zeros((ATOMS, 3), jnp.float32), jnp.arange(GTOT // block_size, dtype=jnp.int32))
    forces = jnp.take(force_all, ordering, axis=0).T
    return density, forces
```

```python
import functools
import math

import jax
import jax.numpy as jnp
import numpy as np
from jax import lax
from jax.experimental import pallas as pl
from jax.experimental.pallas import tpu as pltpu
from jax.sharding import PartitionSpec as P

NPROJ = 18
SPECIES = 2
NL = 9
GRID = 96
LANES = 128

grid_step = 0.0625
highest = lax.Precision.HIGHEST


def group_width():
    return NPROJ * LANES // math.gcd(NPROJ, LANES)


@functools.lru_cache(None)
def gram_tables():
    tiles = group_width() // LANES
    lane = np.arange(LANES)
    same, pick = [], []
    for t in range(tiles):
        rows = t * LANES + lane
        other = np.where(lane < LANES // 2, (t + 1) * LANES + lane, (t - 1) * LANES + lane)
        cols = np.concatenate([rows, other])
        same.append(rows[:, None] // NPROJ == cols[None, :] // NPROJ)
        pick.append(cols[:, None] % NPROJ == lane[None, :])
    return np.stack(same).astype(np.float32), np.stack(pick).astype(np.float32)


@functools.lru_cache(None)
def monomials():
    powers = [
        (i, j, k) for i in range(4) for j in range(4 - i) for k in range(4 - i - j)
    ]
    shapes = [
        {(0, 0, 0): 1.0},
        {(1, 0, 0): 1.0},
        {(0, 1, 0): 1.0},
        {(0, 0, 1): 1.0},
        {(1, 1, 0): 1.0},
        {(0, 1, 1): 1.0},
        {(1, 0, 1): 1.0},
        {(2, 0, 0): 1.0, (0, 2, 0): -1.0},
        {(0, 0, 2): 2.0, (2, 0, 0): -1.0, (0, 2, 0): -1.0},
    ]
    table = np.zeros((4, 16, 3, NL), np.float32)
    for c in range(3):
        for l, terms in enumerate(shapes):
            for power, value in terms.items():
                i, j, k = (p + (axis == c) for axis, p in enumerate(power))
                table[i, j * 4 + k, c, l] += value
    return table


def gram_kernel(occ_ref, weight_ref, x_ref, same_ref, pick_ref, out_ref, rows_ref):
    spin = pl.program_id(0)
    kcount, bcount, width = x_ref.shape[2:]
    tiles = width // LANES
    atoms = width // NPROJ
    band = lax.broadcasted_iota(jnp.int32, (bcount, LANES), 0)
    masks = [
        (band < occ_ref[spin, k]).astype(jnp.float32).astype(jnp.bfloat16)
        for k in range(kcount)
    ]
    low = lax.broadcasted_iota(jnp.int32, (bcount, LANES), 1) < LANES // 2
    for t in range(tiles):
        here = slice(t * LANES, (t + 1) * LANES)
        before = slice(max(t - 1, 0) * LANES, max(t - 1, 0) * LANES + LANES)
        after = slice(min(t + 1, tiles - 1) * LANES, min(t + 1, tiles - 1) * LANES + LANES)
        real, imag = None, None
        for k in range(kcount):
            windows, turned = [], []
            for c in range(2):
                own = x_ref[0, c, k, :, here]
                other = jnp.where(low, x_ref[0, c, k, :, after], x_ref[0, c, k, :, before])
                windows.append(jnp.concatenate([own * masks[k], other * masks[k]], axis=1))
                turned.append(own.T)

            def dot(a, b):
                return jnp.dot(turned[a], windows[b], preferred_element_type=jnp.float32)

            weight = weight_ref[k]
            re = (dot(0, 0) + dot(1, 1)) * weight
            im = (dot(0, 1) - dot(1, 0)) * weight
            real = re if real is None else real + re
            imag = im if imag is None else imag + im
        pick = pick_ref[t]
        for c, value in enumerate((real, imag)):
            value = value * same_ref[t].astype(jnp.float32)
            high = value.astype(jnp.bfloat16)
            rest = (value - high.astype(jnp.float32)).astype(jnp.bfloat16)
            rows_ref[c, here, :] = jnp.dot(
                high, pick, preferred_element_type=jnp.float32
            ) + jnp.dot(rest, pick, preferred_element_type=jnp.float32)
    lane = lax.broadcasted_iota(jnp.int32, (atoms, LANES), 1)
    for c in range(2):
        sums = [None] * (out_ref.shape[3] // LANES)
        for i in range(NPROJ):
            piece = rows_ref[c, pl.ds(i, atoms, stride=NPROJ), :]
            at, offset = divmod(i * NPROJ, LANES)
            if offset:
                piece = pltpu.roll(piece, offset, 1)
            parts = [(at, piece)]
            if offset + NPROJ > LANES:
                parts = [
                    (at, jnp.where(lane >= offset, piece, 0.0)),
                    (at + 1, jnp.where(lane >= offset, 0.0, piece)),
                ]
            for tile, part in parts:
                sums[tile] = part if sums[tile] is None else sums[tile] + part
        for tile, total in enumerate(sums):
            out_ref[0, c, :, tile * LANES : (tile + 1) * LANES] = total


def gram(coefficients, held, kweights):
    spins, parts, kcount, bcount, columns = coefficients.shape
    width = group_width()
    groups = columns // width
    atoms = width // NPROJ
    padded = -(-NPROJ * NPROJ // LANES) * LANES
    same, pick = gram_tables()
    tiles = width // LANES
    return pl.pallas_call(
        gram_kernel,
        grid=(spins, groups),
        out_shape=jax.ShapeDtypeStruct((spins, parts, columns // NPROJ, padded), jnp.float32),
        in_specs=[
            pl.BlockSpec(memory_space=pltpu.SMEM),
            pl.BlockSpec(memory_space=pltpu.SMEM),
            pl.BlockSpec((1, parts, kcount, bcount, width), lambda s, g: (s, 0, 0, 0, g)),
            pl.BlockSpec((tiles, LANES, 2 * LANES), lambda s, g: (0, 0, 0)),
            pl.BlockSpec((tiles, 2 * LANES, LANES), lambda s, g: (0, 0, 0)),
        ],
        out_specs=pl.BlockSpec((1, parts, atoms, padded), lambda s, g: (s, 0, g, 0)),
        scratch_shapes=[pltpu.VMEM((parts, width, LANES), jnp.float32)],
        compiler_params=pltpu.CompilerParams(
            dimension_semantics=("arbitrary", "arbitrary"), vmem_limit_bytes=40 * 2**20
        ),
        cost_estimate=pl.CostEstimate(
            flops=16 * spins * kcount * bcount * columns * 2 * LANES,
            bytes_accessed=coefficients.size * 2,
            transcendentals=0,
        ),
    )(held, kweights, coefficients, jnp.asarray(same, jnp.bfloat16), jnp.asarray(pick, jnp.bfloat16))


def signed_steps(index):
    return grid_step * jnp.where(index >= GRID // 2, index - GRID, index).astype(jnp.float32)


def wave_sums(places, spread, potential, first_plane):
    atoms = places.shape[1]
    planes = potential.shape[1] // (GRID * GRID)
    line = signed_steps(jnp.arange(GRID, dtype=jnp.int32))
    depth = signed_steps(first_plane + jnp.arange(planes, dtype=jnp.int32))

    def factor(axis, steps):
        angle = places[axis][:, None] * steps[None, :]
        damp = jnp.exp(-spread[:, None] * (steps * steps)[None, :])
        return damp * jnp.cos(angle), damp * jnp.sin(angle)

    cos_x, sin_x = factor(0, line)
    cos_y, sin_y = factor(1, line)
    cos_z, sin_z = factor(2, depth)
    power_x = jnp.stack([jnp.ones_like(line), line, line * line, line * line * line])
    left = jnp.stack(
        [
            jnp.concatenate([cos_x, sin_x], axis=1),
            jnp.concatenate([sin_x, -cos_x], axis=1),
        ]
    )
    left = left[:, None] * jnp.concatenate([power_x, power_x], axis=1)[None, :, None, :]
    grid = potential.reshape(2, planes * GRID, GRID)
    right = jnp.concatenate([grid[1], grid[0]], axis=1)
    along = lax.dot_general(
        left.reshape(8 * atoms, 2 * GRID), right, (((1,), (1,)), ((), ())), precision=highest
    ).reshape(2, 4, atoms, planes, GRID)
    cos_yz = cos_z[:, :, None] * cos_y[:, None, :] - sin_z[:, :, None] * sin_y[:, None, :]
    sin_yz = cos_z[:, :, None] * sin_y[:, None, :] + sin_z[:, :, None] * cos_y[:, None, :]
    wave = along[0] * cos_yz[None] - along[1] * sin_yz[None]
    power_z = jnp.stack([jnp.ones_like(depth), depth, depth * depth, depth * depth * depth])
    weights = power_z[None, :, :, None] * power_x[:, None, None, :]
    sums = jnp.dot(
        wave.reshape(4 * atoms, planes * GRID),
        weights.reshape(16, planes * GRID).T,
        precision=highest,
    ).reshape(4, atoms, 16)
    return jnp.einsum("ian,incl->acl", sums, jnp.asarray(monomials()), precision=highest)


def shards(
    coefficients, occupied, kweights, owner_map, species, positions, multipole, widths, potential
):
    spins, parts, kcount, bcount, columns = coefficients.shape
    atoms_blk = columns // NPROJ
    owners = lax.axis_size("ka") * lax.axis_size("ba")
    per_owner = atoms_blk // owners
    owner_index = lax.axis_index(("ka", "ba"))
    group_index = lax.axis_index("ga")
    held = occupied - lax.axis_index("ba") * bcount
    density_local = gram(coefficients, held, kweights)

    owner_rows = owner_map.reshape(-1, atoms_blk)
    blocks = owner_rows.shape[0]
    number = jnp.arange(atoms_blk, dtype=jnp.int32)
    ahead = (owner_rows[:, None, :] == owner_rows[:, :, None]) & (
        number[None, None, :] < number[None, :, None]
    )
    spot = owner_rows * per_owner + jnp.sum(ahead.astype(jnp.int32), axis=2)
    my_spot = lax.dynamic_index_in_dim(spot, group_index, 0, keepdims=False)
    route = (number[:, None] == my_spot[None, :]).astype(jnp.float32)
    routed = jnp.einsum(
        "opa,scae->oscpe", route.reshape(owners, per_owner, atoms_blk), density_local, precision=highest
    )
    own_density = lax.psum_scatter(routed, ("ka", "ba"), scatter_dimension=0, tiled=True)[0]
    own_density = own_density[..., : NPROJ * NPROJ]

    mine = owner_index * per_owner + jnp.arange(per_owner, dtype=jnp.int32)
    chosen = spot[:, None, :] == mine[None, :, None]
    places = jnp.sum(
        jnp.where(chosen[None], positions.reshape(3, blocks, 1, atoms_blk), 0.0), axis=3
    ).reshape(3, -1)
    kinds = jnp.sum(jnp.where(chosen, species.reshape(blocks, 1, atoms_blk), 0), axis=2)
    spread = jnp.where(kinds.reshape(-1) == 0, widths[0], widths[1])
    first_plane = group_index * (potential.shape[1] // (GRID * GRID))
    terms = wave_sums(places, spread, potential, first_plane)
    terms = lax.psum(terms.reshape(blocks, per_owner, 3 * NL), "ga")
    own_terms = lax.dynamic_index_in_dim(terms, group_index, 0, keepdims=False)
    own_kinds = lax.dynamic_index_in_dim(kinds, group_index, 0, keepdims=False)

    real_total = jnp.sum(own_density[:, 0], axis=0)
    moments = jnp.dot(
        real_total, multipole.reshape(SPECIES * NL, NPROJ * NPROJ).T, precision=highest
    ).reshape(per_owner, SPECIES, NL)
    picked = own_kinds[:, None] == jnp.arange(SPECIES, dtype=jnp.int32)[None, :]
    own_moments = jnp.sum(jnp.where(picked[:, :, None], moments, 0.0), axis=1)
    own_force = jnp.sum(own_terms.reshape(per_owner, 3, NL) * own_moments[:, None, :], axis=2)
    return (own_density, own_force.T)


def solution(mesh):
    placed = (
        P(None, None, ("grp", "ka"), "ba", "ga"),
        P(None, ("grp", "ka")),
        P(("grp", "ka")),
        P("grp"),
        P("grp"),
        P(None, "grp"),
        P(),
        P(),
        P(None, ("grp", "ga")),
    )
    return jax.shard_map(
        shards,
        mesh=mesh,
        in_specs=placed,
        out_specs=(
            P(None, None, ("grp", "ka", "ga", "ba"), None),
            P(None, ("grp", "ka", "ga", "ba")),
        ),
        check_vma=False,
    )
```

```python
import functools
import math

import jax
import jax.numpy as jnp
import numpy as np
from jax import lax
from jax.experimental import pallas as pl
from jax.experimental.pallas import tpu as pltpu
from jax.sharding import PartitionSpec as P

NPROJ = 18
SPECIES = 2
NL = 9
GRID = 96
LANES = 128

grid_step = 0.0625
highest = lax.Precision.HIGHEST


def group_width():
    return NPROJ * LANES // math.gcd(NPROJ, LANES)


@functools.lru_cache(None)
def gram_tables():
    tiles = group_width() // LANES
    lane = np.arange(LANES)
    same, pick = [], []
    for t in range(tiles):
        rows = t * LANES + lane
        other = np.where(lane < LANES // 2, (t + 1) * LANES + lane, (t - 1) * LANES + lane)
        cols = np.concatenate([rows, other])
        same.append(rows[:, None] // NPROJ == cols[None, :] // NPROJ)
        pick.append(cols[:, None] % NPROJ == lane[None, :])
    return np.stack(same).astype(np.float32), np.stack(pick).astype(np.float32)


@functools.lru_cache(None)
def monomials():
    powers = [
        (i, j, k) for i in range(4) for j in range(4 - i) for k in range(4 - i - j)
    ]
    shapes = [
        {(0, 0, 0): 1.0},
        {(1, 0, 0): 1.0},
        {(0, 1, 0): 1.0},
        {(0, 0, 1): 1.0},
        {(1, 1, 0): 1.0},
        {(0, 1, 1): 1.0},
        {(1, 0, 1): 1.0},
        {(2, 0, 0): 1.0, (0, 2, 0): -1.0},
        {(0, 0, 2): 2.0, (2, 0, 0): -1.0, (0, 2, 0): -1.0},
    ]
    table = np.zeros((4, 16, 3, NL), np.float32)
    for c in range(3):
        for l, terms in enumerate(shapes):
            for power, value in terms.items():
                i, j, k = (p + (axis == c) for axis, p in enumerate(power))
                table[i, j * 4 + k, c, l] += value
    return table


def gram_kernel(occ_ref, weight_ref, x_ref, same_ref, pick_ref, out_ref, rows_ref):
    spin = pl.program_id(0)
    kcount, bcount, width = x_ref.shape[2:]
    tiles = width // LANES
    atoms = width // NPROJ
    band = lax.broadcasted_iota(jnp.int32, (bcount, LANES), 0)
    masks = [
        (band < occ_ref[spin, k]).astype(jnp.float32).astype(jnp.bfloat16)
        for k in range(kcount)
    ]
    low = lax.broadcasted_iota(jnp.int32, (bcount, LANES), 1) < LANES // 2
    for t in range(tiles):
        here = slice(t * LANES, (t + 1) * LANES)
        before = slice(max(t - 1, 0) * LANES, max(t - 1, 0) * LANES + LANES)
        after = slice(min(t + 1, tiles - 1) * LANES, min(t + 1, tiles - 1) * LANES + LANES)
        real, imag = None, None
        for k in range(kcount):
            windows, turned = [], []
            for c in range(2):
                own = x_ref[0, c, k, :, here]
                other = jnp.where(low, x_ref[0, c, k, :, after], x_ref[0, c, k, :, before])
                windows.append(jnp.concatenate([own * masks[k], other * masks[k]], axis=1))
                turned.append(own.T)

            def dot(a, b):
                return jnp.dot(turned[a], windows[b], preferred_element_type=jnp.float32)

            weight = weight_ref[k]
            re = (dot(0, 0) + dot(1, 1)) * weight
            im = (dot(0, 1) - dot(1, 0)) * weight
            real = re if real is None else real + re
            imag = im if imag is None else imag + im
        pick = pick_ref[t]
        for c, value in enumerate((real, imag)):
            value = value * same_ref[t].astype(jnp.float32)
            high = value.astype(jnp.bfloat16)
            rest = (value - high.astype(jnp.float32)).astype(jnp.bfloat16)
            rows_ref[c, here, :] = jnp.dot(
                high, pick, preferred_element_type=jnp.float32
            ) + jnp.dot(rest, pick, preferred_element_type=jnp.float32)
    lane = lax.broadcasted_iota(jnp.int32, (atoms, LANES), 1)
    for c in range(2):
        sums = [None] * (out_ref.shape[3] // LANES)
        for i in range(NPROJ):
            piece = rows_ref[c, pl.ds(i, atoms, stride=NPROJ), :]
            at, offset = divmod(i * NPROJ, LANES)
            if offset:
                piece = pltpu.roll(piece, offset, 1)
            parts = [(at, piece)]
            if offset + NPROJ > LANES:
                parts = [
                    (at, jnp.where(lane >= offset, piece, 0.0)),
                    (at + 1, jnp.where(lane >= offset, 0.0, piece)),
                ]
            for tile, part in parts:
                sums[tile] = part if sums[tile] is None else sums[tile] + part
        for tile, total in enumerate(sums):
            out_ref[0, c, :, tile * LANES : (tile + 1) * LANES] = total


def gram(coefficients, held, kweights):
    spins, parts, kcount, bcount, columns = coefficients.shape
    width = group_width()
    groups = columns // width
    atoms = width // NPROJ
    padded = -(-NPROJ * NPROJ // LANES) * LANES
    same, pick = gram_tables()
    tiles = width // LANES
    return pl.pallas_call(
        gram_kernel,
        grid=(spins, groups),
        out_shape=jax.ShapeDtypeStruct((spins, parts, columns // NPROJ, padded), jnp.float32),
        in_specs=[
            pl.BlockSpec(memory_space=pltpu.SMEM),
            pl.BlockSpec(memory_space=pltpu.SMEM),
            pl.BlockSpec((1, parts, kcount, bcount, width), lambda s, g: (s, 0, 0, 0, g)),
            pl.BlockSpec((tiles, LANES, 2 * LANES), lambda s, g: (0, 0, 0)),
            pl.BlockSpec((tiles, 2 * LANES, LANES), lambda s, g: (0, 0, 0)),
        ],
        out_specs=pl.BlockSpec((1, parts, atoms, padded), lambda s, g: (s, 0, g, 0)),
        scratch_shapes=[pltpu.VMEM((parts, width, LANES), jnp.float32)],
        compiler_params=pltpu.CompilerParams(
            dimension_semantics=("arbitrary", "arbitrary"), vmem_limit_bytes=40 * 2**20
        ),
        cost_estimate=pl.CostEstimate(
            flops=16 * spins * kcount * bcount * columns * 2 * LANES,
            bytes_accessed=coefficients.size * 2,
            transcendentals=0,
        ),
    )(held, kweights, coefficients, jnp.asarray(same, jnp.bfloat16), jnp.asarray(pick, jnp.bfloat16))


def gather_kernel(
    rows_ref, terms_ref, total_ref, sum_ref, first, held, second, third,
    send1, recv1, send2, recv2, send3, recv3,
):
    mesh_id = pl.DeviceIdType.MESH
    ka, ba, ga = (lax.axis_size(name) for name in ("ka", "ba", "ga"))
    k, b, g = (lax.axis_index(name) for name in ("ka", "ba", "ga"))
    barrier = pltpu.get_barrier_semaphore()
    for name, me, size in (("ka", k, ka), ("ba", b, ba), ("ga", g, ga)):
        for step in range(1, size):
            pl.semaphore_signal(
                barrier, inc=1, device_id={name: lax.rem(me + step, size)}, device_id_type=mesh_id
            )
    pl.semaphore_wait(barrier, ka + ba + ga - 3)

    copies1, copies2, copies3 = {}, {}, {}
    for turn in list(range(1, ka)) + [0]:
        to = lax.rem(k + turn, ka)
        for step in range(1, ba):
            peer = lax.rem(b + step, ba)
            copy = pltpu.make_async_remote_copy(
                src_ref=rows_ref.at[to, peer],
                dst_ref=first.at[step - 1, turn],
                send_sem=send1.at[step - 1, turn],
                recv_sem=recv1.at[step - 1, turn],
                device_id={"ba": peer},
                device_id_type=mesh_id,
            )
            copy.start()
            copies1[turn, step] = copy
    for step in range(1, ga):
        peer = lax.rem(g + step, ga)
        copy = pltpu.make_async_remote_copy(
            src_ref=terms_ref.at[peer],
            dst_ref=third.at[step - 1],
            send_sem=send3.at[step - 1],
            recv_sem=recv3.at[step - 1],
            device_id={"ga": peer},
            device_id_type=mesh_id,
        )
        copy.start()
        copies3[step] = copy
    for turn in range(1, ka):
        to = lax.rem(k + turn, ka)
        value = rows_ref[to, b]
        for step in range(1, ba):
            copies1[turn, step].wait_recv()
            value = value + first[step - 1, turn]
        held[turn - 1] = value
        copy = pltpu.make_async_remote_copy(
            src_ref=held.at[turn - 1],
            dst_ref=second.at[turn - 1],
            send_sem=send2.at[turn - 1],
            recv_sem=recv2.at[turn - 1],
            device_id={"ka": to},
            device_id_type=mesh_id,
        )
        copy.start()
        copies2[turn] = copy
    value = rows_ref[k, b]
    for step in range(1, ba):
        copies1[0, step].wait_recv()
        value = value + first[step - 1, 0]
    terms = terms_ref[g]
    for step in range(1, ga):
        copies3[step].wait_recv()
        terms = terms + third[step - 1]
    sum_ref[...] = terms
    for turn in range(1, ka):
        copies2[turn].wait_recv()
        value = value + second[turn - 1]
    total_ref[...] = value
    for copy in [*copies1.values(), *copies2.values(), *copies3.values()]:
        copy.wait_send()


def gather_sums(rows, terms):
    ka, ba = rows.shape[:2]
    chunk, piece = rows.shape[2:], terms.shape[1:]
    ga = lax.axis_size("ga")
    vmem = pl.BlockSpec(memory_space=pltpu.VMEM)
    return pl.pallas_call(
        gather_kernel,
        out_shape=(
            jax.ShapeDtypeStruct(chunk, jnp.float32),
            jax.ShapeDtypeStruct(piece, jnp.float32),
        ),
        in_specs=[vmem, vmem],
        out_specs=(vmem, vmem),
        scratch_shapes=[
            pltpu.VMEM((ba - 1, ka, *chunk), jnp.float32),
            pltpu.VMEM((ka - 1, *chunk), jnp.float32),
            pltpu.VMEM((ka - 1, *chunk), jnp.float32),
            pltpu.VMEM((ga - 1, *piece), jnp.float32),
            pltpu.SemaphoreType.DMA((ba - 1, ka)),
            pltpu.SemaphoreType.DMA((ba - 1, ka)),
            pltpu.SemaphoreType.DMA((ka - 1,)),
            pltpu.SemaphoreType.DMA((ka - 1,)),
            pltpu.SemaphoreType.DMA((ga - 1,)),
            pltpu.SemaphoreType.DMA((ga - 1,)),
        ],
        compiler_params=pltpu.CompilerParams(collective_id=0, has_side_effects=True),
    )(rows, terms)


def signed_steps(index):
    return grid_step * jnp.where(index >= GRID // 2, index - GRID, index).astype(jnp.float32)


def wave_sums(places, spread, potential, first_plane):
    atoms = places.shape[1]
    planes = potential.shape[1] // (GRID * GRID)
    line = signed_steps(jnp.arange(GRID, dtype=jnp.int32))
    depth = signed_steps(first_plane + jnp.arange(planes, dtype=jnp.int32))

    def factor(axis, steps):
        angle = places[axis][:, None] * steps[None, :]
        damp = jnp.exp(-spread[:, None] * (steps * steps)[None, :])
        return damp * jnp.cos(angle), damp * jnp.sin(angle)

    cos_x, sin_x = factor(0, line)
    cos_y, sin_y = factor(1, line)
    cos_z, sin_z = factor(2, depth)
    power_x = jnp.stack([jnp.ones_like(line), line, line * line, line * line * line])
    left = jnp.stack(
        [
            jnp.concatenate([cos_x, sin_x], axis=1),
            jnp.concatenate([sin_x, -cos_x], axis=1),
        ]
    )
    left = left[:, None] * jnp.concatenate([power_x, power_x], axis=1)[None, :, None, :]
    grid = potential.reshape(2, planes * GRID, GRID)
    right = jnp.concatenate([grid[1], grid[0]], axis=1)
    along = lax.dot_general(
        left.reshape(8 * atoms, 2 * GRID), right, (((1,), (1,)), ((), ())), precision=highest
    ).reshape(2, 4, atoms, planes, GRID)
    cos_yz = cos_z[:, :, None] * cos_y[:, None, :] - sin_z[:, :, None] * sin_y[:, None, :]
    sin_yz = cos_z[:, :, None] * sin_y[:, None, :] + sin_z[:, :, None] * cos_y[:, None, :]
    wave = along[0] * cos_yz[None] - along[1] * sin_yz[None]
    power_z = jnp.stack([jnp.ones_like(depth), depth, depth * depth, depth * depth * depth])
    weights = power_z[None, :, :, None] * power_x[:, None, None, :]
    sums = jnp.dot(
        wave.reshape(4 * atoms, planes * GRID),
        weights.reshape(16, planes * GRID).T,
        precision=highest,
    ).reshape(4, atoms, 16)
    return jnp.einsum("ian,incl->acl", sums, jnp.asarray(monomials()), precision=highest)


def shards(
    coefficients, occupied, kweights, owner_map, species, positions, multipole, widths, potential
):
    spins, parts, kcount, bcount, columns = coefficients.shape
    atoms_blk = columns // NPROJ
    owners = lax.axis_size("ka") * lax.axis_size("ba")
    per_owner = atoms_blk // owners
    owner_index = lax.axis_index(("ka", "ba"))
    group_index = lax.axis_index("ga")
    held = occupied - lax.axis_index("ba") * bcount
    density_local = gram(coefficients, held, kweights)

    owner_rows = owner_map.reshape(-1, atoms_blk)
    blocks = owner_rows.shape[0]
    number = jnp.arange(atoms_blk, dtype=jnp.int32)
    ahead = (owner_rows[:, None, :] == owner_rows[:, :, None]) & (
        number[None, None, :] < number[None, :, None]
    )
    spot = owner_rows * per_owner + jnp.sum(ahead.astype(jnp.int32), axis=2)
    my_spot = lax.dynamic_index_in_dim(spot, group_index, 0, keepdims=False)
    route = (number[:, None] == my_spot[None, :]).astype(jnp.float32)
    routed = jnp.einsum(
        "opa,scae->oscpe", route.reshape(owners, per_owner, atoms_blk), density_local, precision=highest
    )
    mine = owner_index * per_owner + jnp.arange(per_owner, dtype=jnp.int32)
    chosen = spot[:, None, :] == mine[None, :, None]
    places = jnp.sum(
        jnp.where(chosen[None], positions.reshape(3, blocks, 1, atoms_blk), 0.0), axis=3
    ).reshape(3, -1)
    kinds = jnp.sum(jnp.where(chosen, species.reshape(blocks, 1, atoms_blk), 0), axis=2)
    spread = jnp.where(kinds.reshape(-1) == 0, widths[0], widths[1])
    first_plane = group_index * (potential.shape[1] // (GRID * GRID))
    terms = wave_sums(places, spread, potential, first_plane)
    terms = terms.reshape(blocks, per_owner, 3 * NL)
    terms = jnp.pad(terms, ((0, 0), (0, 0), (0, -3 * NL % LANES)))
    rows = routed.reshape(
        lax.axis_size("ka"), lax.axis_size("ba"), spins * parts, per_owner, routed.shape[-1]
    )
    total, own_terms = gather_sums(rows, terms)
    own_density = total.reshape(spins, parts, per_owner, -1)[..., : NPROJ * NPROJ]
    own_terms = own_terms[:, : 3 * NL]
    own_kinds = lax.dynamic_index_in_dim(kinds, group_index, 0, keepdims=False)

    real_total = jnp.sum(own_density[:, 0], axis=0)
    moments = jnp.dot(
        real_total, multipole.reshape(SPECIES * NL, NPROJ * NPROJ).T, precision=highest
    ).reshape(per_owner, SPECIES, NL)
    picked = own_kinds[:, None] == jnp.arange(SPECIES, dtype=jnp.int32)[None, :]
    own_moments = jnp.sum(jnp.where(picked[:, :, None], moments, 0.0), axis=1)
    own_force = jnp.sum(own_terms.reshape(per_owner, 3, NL) * own_moments[:, None, :], axis=2)
    return (own_density, own_force.T)


def solution(mesh):
    placed = (
        P(None, None, ("grp", "ka"), "ba", "ga"),
        P(None, ("grp", "ka")),
        P(("grp", "ka")),
        P("grp"),
        P("grp"),
        P(None, "grp"),
        P(),
        P(),
        P(None, ("grp", "ga")),
    )
    return jax.shard_map(
        shards,
        mesh=mesh,
        in_specs=placed,
        out_specs=(
            P(None, None, ("grp", "ka", "ga", "ba"), None),
            P(None, ("grp", "ka", "ga", "ba")),
        ),
        check_vma=False,
    )
```
